32 devices in a mesh: replica: 16 (over z, y, x), shard: 2 (over core).
Axes of the slice: x: 2, y: 2, z: 4, core: 2. Of those that a mesh axis runs over, the one named last changes fastest.
Arguments:
- hidden_in: bfloat16 [4096, 1024], P(('replica', 'shard')), may hold values from -6 to 6
- segment_ids: int32 [32, 128], P(('replica', 'shard')), may hold values from 0 to 15, never falling along the last dimension, each value on 1 to 64 neighbouring positions
- cotangent: bfloat16 [4096, 1024], P(('replica', 'shard')), may hold values from -6 to 6
- attention_norm_gain: bfloat16 [1024], P('shard'), may hold values from 0.25 to 1.75
- attention_norm_bias: bfloat16 [1024], P('shard'), may hold values from -3 to 3
- feedforward_norm_gain: bfloat16 [1024], P('shard'), may hold values from 0.25 to 1.75
- feedforward_norm_bias: bfloat16 [1024], P('shard'), may hold values from -3 to 3
- w_qkv: bfloat16 [1024, 3072], P('shard'), may hold values from -0.1875 to 0.1875
- b_qkv: bfloat16 [3072], P('shard'), may hold values from -3 to 3
- w_out: bfloat16 [1024, 1024], P('shard'), may hold values from -0.4375 to 0.4375
- b_out: bfloat16 [1024], P('shard'), may hold values from -3 to 3
- w_up: bfloat16 [1024, 4096], P('shard'), may hold values from -0.1875 to 0.1875
- b_up: bfloat16 [4096], P('shard'), may hold values from -3 to 3
- w_down: bfloat16 [4096, 1024], P('shard'), may hold values from -0.125 to 0.125
- b_down: bfloat16 [1024], P('shard'), may hold values from -3 to 3
Outputs:
- hidden_out: bfloat16 [4096, 1024], P(('replica', 'shard'))
- grad_in: bfloat16 [4096, 1024], P(('replica', 'shard'))
- grad_ln1_gain: float32 [1024], P('shard')
- grad_ln1_bias: float32 [1024], P('shard')
- grad_ln2_gain: float32 [1024], P('shard')
- grad_ln2_bias: float32 [1024], P('shard')
- grad_w_qkv: float32 [1024, 3072], P('shard')
- grad_b_qkv: float32 [3072], P('shard')
- grad_w_out: float32 [1024, 1024], P('shard')
- grad_b_out: float32 [1024], P('shard')
- grad_w_up: float32 [1024, 4096], P('shard')
- grad_b_up: float32 [4096], P('shard')
- grad_w_down: float32 [4096, 1024], P('shard')
- grad_b_down: float32 [1024], P('shard')
The draws below stay inside these ranges and needn't reach their ends.
Inputs may be any that keep to these rules, and one draw needn't show every extreme that they name: `segment_ids`: in each device's row, ids never fall from one token to the next; every id occurs; every sequence has 1 to 64 tokens and one has exactly 64.
All inputs are finite; a program needn't handle non-finite values.
Results may differ from the reference program's by a relative error of at most 0.015.
Values may be sent and summed in bfloat16 or wider, within the bound.
A program may use at most 192 MiB of HBM per device.

```python
import math
import jax
import jax.numpy as jnp
import numpy as np
from jax import lax

D = 1024
HEADS = 16
FF = 4096
TOK_DEV = 128
SEQ_MOST = 64
SEQ_COUNT = 16
TOKENS = 4096
DEVICES = 32


def level_of(own_key, shape, shards, smallest, high):
    level = 1.0
    for axis_at, shards_of in shards:
        steps = jax.random.uniform(jax.random.fold_in(jax.random.fold_in(own_key, 6), axis_at), (shards_of,), jnp.float32, smallest / len(shards), high / len(shards))
        level = level * jnp.repeat(jnp.exp(steps), shape[axis_at] // shards_of).reshape((-1,) + (1,) * (len(shape) - 1 - axis_at))
    return level


def length_profile(number_of, total, reach, skew):
    portions = [(1 << 20) // math.isqrt(rank ** skew) + 1 for rank in range(2, number_of + 1)]
    rest, holding = total - reach - (number_of - 1), [1] * (number_of - 1)
    while rest > 0:
        movable = [i for i in range(number_of - 1) if holding[i] < reach]
        mass, budget = sum([portions[i] for i in movable]), rest
        for i in movable:
            more = min(reach - holding[i], max(1, budget * portions[i] // mass), rest)
            holding[i] = holding[i] + more
            rest = rest - more
    return np.array([reach] + holding)


def ragged_sizes(rng, amount, total, bound, skew):
    if amount == 2:
        one = jax.random.randint(rng, (), max(1, total - bound), min(bound, total - 1) + 1)
        return jnp.stack([one, total - one])
    lengths = jnp.asarray(length_profile(amount, total, bound, skew), jnp.int32)
    twos = (amount - 1) // 2
    giver, taker = lengths[1:1 + 2 * twos:2], lengths[2:2 + 2 * twos:2]
    slack = jnp.minimum(giver - 1, bound - taker)
    shifted = jax.random.randint(jax.random.fold_in(rng, 1), (twos,), 0, 1 << 20) % (slack + 1)
    lengths = lengths.at[1:1 + 2 * twos:2].set(giver - shifted).at[2:2 + 2 * twos:2].set(taker + shifted)
    return lengths[jax.random.permutation(jax.random.fold_in(rng, 2), amount)]


def normal_values(own_key, shape, scale, reach, shards=(), held_as=jnp.bfloat16):
    result = jax.random.normal(own_key, shape, jnp.float32) * scale
    if len(shards) > 0:
        result = level_of(own_key, shape, shards, -0.22, 0.18) * result
    return jnp.clip(result, min=-reach, max=reach).astype(held_as)


def setup_inputs(seed: int = 0) -> dict:
    arg_keys = jax.random.split(jax.random.key(seed), 16)
    hidden_in = normal_values(arg_keys[0], (TOKENS, D), 1.0, 6.0, ((0, 32),))
    segment_ids = jax.vmap(lambda own: jnp.searchsorted(jnp.cumsum(ragged_sizes(own, SEQ_COUNT, TOK_DEV, SEQ_MOST, 2)), jnp.arange(TOK_DEV), side="right"))(jax.random.split(arg_keys[1], DEVICES)).reshape((DEVICES, TOK_DEV)).astype(jnp.int32)
    cotangent = normal_values(arg_keys[2], (TOKENS, D), 1.0, 6.0, ((0, 32),))
    attention_norm_gain = jnp.clip(1.0 + 0.15 * jax.random.normal(arg_keys[3], (D,), jnp.float32), 0.25, 1.75).astype(jnp.bfloat16)
    attention_norm_bias = normal_values(arg_keys[4], (D,), 0.5, 3.0, ((0, 2),))
    feedforward_norm_gain = jnp.clip(1.0 + 0.15 * jax.random.normal(arg_keys[5], (D,), jnp.float32), 0.25, 1.75).astype(jnp.bfloat16)
    feedforward_norm_bias = normal_values(arg_keys[6], (D,), 0.5, 3.0, ((0, 2),))
    w_qkv = normal_values(arg_keys[7], (D, 3 * D), D ** -0.5, 0.1875, ((0, 2),))
    b_qkv = normal_values(arg_keys[8], (3 * D,), 0.5, 3.0, ((0, 2),))
    w_out = normal_values(arg_keys[9], (D, D), (D // 6) ** -0.5, 0.4375, ((0, 2),))
    b_out = normal_values(arg_keys[10], (D,), 0.5, 3.0, ((0, 2),))
    w_up = normal_values(arg_keys[11], (D, FF), D ** -0.5, 0.1875, ((0, 2),))
    b_up = normal_values(arg_keys[12], (FF,), 0.5, 3.0, ((0, 2),))
    w_down = normal_values(arg_keys[13], (FF, D), (FF // 2) ** -0.5, 0.125, ((0, 2),))
    b_down = normal_values(arg_keys[14], (D,), 0.5, 3.0, ((0, 2),))
    return {"hidden_in": hidden_in, "segment_ids": segment_ids, "cotangent": cotangent, "attention_norm_gain": attention_norm_gain, "attention_norm_bias": attention_norm_bias, "feedforward_norm_gain": feedforward_norm_gain, "feedforward_norm_bias": feedforward_norm_bias, "w_qkv": w_qkv, "b_qkv": b_qkv, "w_out": w_out, "b_out": b_out, "w_up": w_up, "b_up": b_up, "w_down": w_down, "b_down": b_down}


def layer_normalize(input_widened, gain, shift):
    center = input_widened - lax.optimization_barrier(jnp.mean(input_widened, axis=-1, keepdims=True))
    spread = lax.optimization_barrier(jnp.mean(center * center, axis=-1, keepdims=True))
    inv_std = lax.rsqrt(spread + 1e-05)
    x_hat = center * inv_std
    return (x_hat * gain.astype(jnp.float32) + shift.astype(jnp.float32), x_hat, inv_std)

def seq_tables(seg_row, rot_dims):
    count = seg_row.shape[0]
    index = jnp.arange(count, dtype=jnp.int32)
    same_seg = seg_row[:, None] == seg_row[None, :]
    first = lax.optimization_barrier(jnp.min(jnp.where(same_seg, index[None, :], count), axis=1))
    position = (index - first).astype(jnp.float32)
    allowed = same_seg & (index[None, :] <= index[:, None])
    half = rot_dims // 2
    freqs = 10000.0 ** (-(2.0 * jnp.arange(half, dtype=jnp.float32)) / rot_dims)
    angles = position[:, None] * freqs[None, :]
    return (allowed, jnp.cos(angles)[:, None, :], jnp.sin(angles)[:, None, :])

def rotate(tensor, cosine, sine, rot_dims):
    half = rot_dims // 2
    first_half = tensor[..., :half]
    second_half = tensor[..., half:rot_dims]
    return jnp.concatenate([first_half * cosine - second_half * sine, second_half * cosine + first_half * sine, tensor[..., rot_dims:]], axis=-1)

def unrotate(tensor, cosine, sine, rot_dims):
    half = rot_dims // 2
    first_half = tensor[..., :half]
    second_half = tensor[..., half:rot_dims]
    return jnp.concatenate([first_half * cosine + second_half * sine, second_half * cosine - first_half * sine, tensor[..., rot_dims:]], axis=-1)

def gelu_value(pre_act):
    return pre_act * 0.5 * (1.0 + lax.erf(pre_act * (1.0 / math.sqrt(2.0))))

def gelu_slope(pre_act):
    cdf_part = 0.5 * (1.0 + lax.erf(pre_act * (1.0 / math.sqrt(2.0))))
    pdf_part = jnp.exp(-0.5 * pre_act * pre_act) * (1.0 / math.sqrt(2.0 * math.pi))
    return cdf_part + pre_act * pdf_part

def ein(form, left, right):
    return jnp.einsum(form, left.astype(jnp.float32), right.astype(jnp.float32), precision=lax.Precision.HIGHEST)

def layer_pass(params, tokens_in, seg_row, cot_rows):
    attention_norm_gain, attention_norm_bias, feedforward_norm_gain, feedforward_norm_bias, w_qkv, b_qkv, w_out, b_out, w_up, b_up, w_down, b_down = params
    count, width = tokens_in.shape
    head_dim = width // HEADS
    rot_dims = head_dim // 4
    scale = 1.0 / math.sqrt(head_dim)
    input_widened = tokens_in.astype(jnp.float32)
    attention_normed, attention_centered_scaled, attention_inverse_deviation = layer_normalize(input_widened, attention_norm_gain, attention_norm_bias)
    feedforward_normed, feedforward_centered_scaled, feedforward_inverse_deviation = layer_normalize(input_widened, feedforward_norm_gain, feedforward_norm_bias)
    act_one = attention_normed.astype(jnp.bfloat16)
    act_two = feedforward_normed.astype(jnp.bfloat16)
    allowed, cosine, sine = seq_tables(seg_row, rot_dims)
    qkv = jnp.dot(act_one, w_qkv, preferred_element_type=jnp.float32) + b_qkv.astype(jnp.float32)
    query = qkv[:, :width].reshape(count, HEADS, head_dim)
    keys = qkv[:, width:2 * width].reshape(count, HEADS, head_dim)
    values = qkv[:, 2 * width:].reshape(count, HEADS, head_dim)
    query_rot = rotate(query, cosine, sine, rot_dims).astype(jnp.bfloat16)
    keys_rot = rotate(keys, cosine, sine, rot_dims).astype(jnp.bfloat16)
    values_b = values.astype(jnp.bfloat16)
    scores = ein('qhd,khd->hqk', query_rot, keys_rot) * scale
    masked = jnp.where(allowed[None], scores, -1e+30)
    row_top = lax.optimization_barrier(jnp.max(masked, axis=-1, keepdims=True))
    expd = jnp.where(allowed[None], jnp.exp(masked - row_top), 0.0)
    total = lax.optimization_barrier(jnp.sum(expd, axis=-1, keepdims=True))
    log_sum = row_top + jnp.log(total)
    probs = (expd / total).astype(jnp.bfloat16)
    context = ein('hqk,khd->qhd', probs, values_b).reshape(count, width).astype(jnp.bfloat16)
    attn = jnp.dot(context, w_out, preferred_element_type=jnp.float32) + b_out.astype(jnp.float32)
    pre_act = jnp.dot(act_two, w_up, preferred_element_type=jnp.float32) + b_up.astype(jnp.float32)
    hidden = gelu_value(pre_act).astype(jnp.bfloat16)
    mlp_out = jnp.dot(hidden, w_down, preferred_element_type=jnp.float32) + b_down.astype(jnp.float32)
    out_rows = (input_widened + attn + mlp_out).astype(jnp.bfloat16)
    cot_float = cot_rows.astype(jnp.float32)
    g_w_down = jnp.dot(hidden.T, cot_rows, preferred_element_type=jnp.float32)
    g_b_down = lax.optimization_barrier(jnp.sum(cot_float, axis=0))
    g_w_out = jnp.dot(context.T, cot_rows, preferred_element_type=jnp.float32)
    g_b_out = lax.optimization_barrier(jnp.sum(cot_float, axis=0))
    d_hidden = jnp.dot(cot_rows, w_down.T, preferred_element_type=jnp.float32)
    d_pre = d_hidden * gelu_slope(pre_act)
    d_pre_b = d_pre.astype(jnp.bfloat16)
    g_w_up = jnp.dot(act_two.T, d_pre_b, preferred_element_type=jnp.float32)
    g_b_up = lax.optimization_barrier(jnp.sum(d_pre, axis=0))
    feedforward_norm_gradient = jnp.dot(d_pre_b, w_up.T, preferred_element_type=jnp.float32)
    d_context = jnp.dot(cot_rows, w_out.T, preferred_element_type=jnp.float32).astype(jnp.bfloat16).reshape(count, HEADS, head_dim)
    probs_f = jnp.where(allowed[None], jnp.exp(masked - log_sum), 0.0)
    probs_b = probs_f.astype(jnp.bfloat16)
    d_values = ein('hqk,qhd->khd', probs_b, d_context)
    d_probs = ein('qhd,khd->hqk', d_context, values_b)
    delta = lax.optimization_barrier(jnp.sum(probs_f * d_probs, axis=-1, keepdims=True))
    d_scores = (probs_f * (d_probs - delta) * scale).astype(jnp.bfloat16)
    d_query_rot = ein('hqk,khd->qhd', d_scores, keys_rot)
    d_keys_rot = ein('hqk,qhd->khd', d_scores, query_rot)
    d_query = unrotate(d_query_rot, cosine, sine, rot_dims)
    d_keys = unrotate(d_keys_rot, cosine, sine, rot_dims)
    d_qkv_f = jnp.concatenate([d_query.reshape(count, width), d_keys.reshape(count, width), d_values.reshape(count, width)], axis=1)
    d_qkv = d_qkv_f.astype(jnp.bfloat16)
    g_w_qkv = jnp.dot(act_one.T, d_qkv, preferred_element_type=jnp.float32)
    g_b_qkv = lax.optimization_barrier(jnp.sum(d_qkv_f, axis=0))
    attention_norm_gradient = jnp.dot(d_qkv, w_qkv.T, preferred_element_type=jnp.float32)

    def normalize_backward(d_act, x_hat, inv_std, gain):
        scaled = d_act * gain.astype(jnp.float32)
        d_in = (scaled - lax.optimization_barrier(jnp.mean(scaled, axis=-1, keepdims=True)) - x_hat * lax.optimization_barrier(jnp.mean(scaled * x_hat, axis=-1, keepdims=True))) * inv_std
        return (d_in, lax.optimization_barrier(jnp.sum(d_act * x_hat, axis=0)), lax.optimization_barrier(jnp.sum(d_act, axis=0)))
    attention_input_gradient, attention_norm_gain_gradient, attention_norm_bias_gradient = normalize_backward(attention_norm_gradient, attention_centered_scaled, attention_inverse_deviation, attention_norm_gain)
    feedforward_input_gradient, feedforward_norm_gain_gradient, feedforward_norm_bias_gradient = normalize_backward(feedforward_norm_gradient, feedforward_centered_scaled, feedforward_inverse_deviation, feedforward_norm_gain)
    grad_rows = (cot_float + attention_input_gradient + feedforward_input_gradient).astype(jnp.bfloat16)
    grads = (attention_norm_gain_gradient, attention_norm_bias_gradient, feedforward_norm_gain_gradient, feedforward_norm_bias_gradient, g_w_qkv, g_b_qkv, g_w_out, g_b_out, g_w_up, g_b_up, g_w_down, g_b_down)
    return (out_rows, grad_rows, grads)

def reference(hidden_in, segment_ids, cotangent, attention_norm_gain, attention_norm_bias, feedforward_norm_gain, feedforward_norm_bias, w_qkv, b_qkv, w_out, b_out, w_up, b_up, w_down, b_down):
    params = (attention_norm_gain, attention_norm_bias, feedforward_norm_gain, feedforward_norm_bias, w_qkv, b_qkv, w_out, b_out, w_up, b_up, w_down, b_down)
    blocks = segment_ids.shape[0]
    tokens_in = hidden_in.reshape(blocks, TOK_DEV, D)
    cot_blocks = cotangent.reshape(blocks, TOK_DEV, D)
    start = tuple((jnp.zeros(p.shape, jnp.float32) for p in params))

    def step(carry, item):
        rows, seg_row, cot_rows = item
        out_rows, grad_rows, grads = layer_pass(params, rows, seg_row, cot_rows)
        rounded = tuple((lax.optimization_barrier(g.astype(jnp.bfloat16)).astype(jnp.float32) for g in grads))
        return (tuple((c + g for c, g in zip(carry, rounded))), (out_rows, grad_rows))
    sums, (outs, grad_outs) = lax.scan(step, start, (tokens_in, segment_ids, cot_blocks))
    factor = 1.0 / math.sqrt(TOKENS)
    scaled = [s * factor for s in sums]
    return (outs.reshape(TOKENS, D), grad_outs.reshape(TOKENS, D), scaled[0], scaled[1], scaled[2], scaled[3], scaled[4], scaled[5], scaled[6], scaled[7], scaled[8], scaled[9], scaled[10], scaled[11])
```

```python
import math

import jax
import jax.numpy as jnp
from jax import lax
from jax.sharding import PartitionSpec as P

HEADS = 16


def layer_normalize(input_widened, gain, shift):
    center = input_widened - jnp.mean(input_widened, axis=-1, keepdims=True)
    spread = jnp.mean(center * center, axis=-1, keepdims=True)
    inv_std = lax.rsqrt(spread + 1e-05)
    x_hat = center * inv_std
    return (x_hat * gain.astype(jnp.float32) + shift.astype(jnp.float32), x_hat, inv_std)


def seq_tables(seg_row, rot_dims):
    count = seg_row.shape[0]
    index = jnp.arange(count, dtype=jnp.int32)
    same_seg = seg_row[:, None] == seg_row[None, :]
    first = jnp.min(jnp.where(same_seg, index[None, :], count), axis=1)
    position = (index - first).astype(jnp.float32)
    allowed = same_seg & (index[None, :] <= index[:, None])
    half = rot_dims // 2
    freqs = 10000.0 ** (-(2.0 * jnp.arange(half, dtype=jnp.float32)) / rot_dims)
    angles = position[:, None] * freqs[None, :]
    return (allowed, jnp.cos(angles)[:, None, :], jnp.sin(angles)[:, None, :])


def rotate(tensor, cosine, sine, rot_dims):
    half = rot_dims // 2
    first_half = tensor[..., :half]
    second_half = tensor[..., half:rot_dims]
    return jnp.concatenate(
        [
            first_half * cosine - second_half * sine,
            second_half * cosine + first_half * sine,
            tensor[..., rot_dims:],
        ],
        axis=-1,
    )


def unrotate(tensor, cosine, sine, rot_dims):
    half = rot_dims // 2
    first_half = tensor[..., :half]
    second_half = tensor[..., half:rot_dims]
    return jnp.concatenate(
        [
            first_half * cosine + second_half * sine,
            second_half * cosine - first_half * sine,
            tensor[..., rot_dims:],
        ],
        axis=-1,
    )


def gelu_value(pre_act):
    return pre_act * 0.5 * (1.0 + lax.erf(pre_act * (1.0 / math.sqrt(2.0))))


def gelu_slope(pre_act):
    cdf_part = 0.5 * (1.0 + lax.erf(pre_act * (1.0 / math.sqrt(2.0))))
    pdf_part = jnp.exp(-0.5 * pre_act * pre_act) * (1.0 / math.sqrt(2.0 * math.pi))
    return cdf_part + pre_act * pdf_part


def ein(form, left, right):
    return jnp.einsum(form, left, right, preferred_element_type=jnp.float32)


def normalize_backward(d_act, x_hat, inv_std, gain):
    scaled = d_act * gain.astype(jnp.float32)
    d_in = (
        scaled
        - jnp.mean(scaled, axis=-1, keepdims=True)
        - x_hat * jnp.mean(scaled * x_hat, axis=-1, keepdims=True)
    ) * inv_std
    return (d_in, jnp.sum(d_act * x_hat, axis=0), jnp.sum(d_act, axis=0))


def flip(value, axis, mask):
    size = lax.axis_size(axis)
    return lax.ppermute(value, axis, [(i, i ^ mask) for i in range(size)])


def from_group(value):
    return [value] + [flip(value, "shard", k) for k in range(1, lax.axis_size("shard"))]


def column_piece(value, k, pieces):
    width = value.shape[1] // pieces
    start = (lax.axis_index("shard") ^ k) * width
    return lax.dynamic_slice_in_dim(value, start, width, axis=1)


def to_owners(value):
    pieces = lax.axis_size("shard")
    return [column_piece(value, 0, pieces)] + [
        flip(column_piece(value, k, pieces), "shard", k) for k in range(1, pieces)
    ]


def place(pieces, axis):
    me = lax.axis_index("shard")
    if len(pieces) == 1:
        return pieces[0]
    if len(pieces) == 2:
        return jnp.where(
            me == 0,
            jnp.concatenate(pieces, axis=axis),
            jnp.concatenate(pieces[::-1], axis=axis),
        )
    width = pieces[0].shape[axis]
    shape = list(pieces[0].shape)
    shape[axis] = width * len(pieces)
    whole = jnp.zeros(shape, pieces[0].dtype)
    for k, piece in enumerate(pieces):
        whole = lax.dynamic_update_slice_in_dim(whole, piece, (me ^ k) * width, axis=axis)
    return whole


def rows_dot(act, weights):
    total = None
    for k, piece in enumerate(weights):
        part = ein("td,dc->tc", column_piece(act, k, len(weights)), piece)
        total = part if total is None else total + part
    return total


def back_dot(grad, weights):
    return place([ein("tc,dc->td", grad, piece) for piece in weights], 1)


def owned_grad(left, right):
    return ein(
        "td,tc->dc", jnp.concatenate(left, axis=0), jnp.concatenate(right, axis=0)
    ).astype(jnp.bfloat16)


def bit_orders():
    bits = (lax.axis_size("replica") - 1).bit_length()
    first = list(range(bits))
    second = first[1:] + first[:1]
    return (first, second)


def reduce_rows(part, order):
    me = lax.axis_index("replica")
    for b in order:
        bit = (me >> b) & 1
        halves = part.reshape(2, part.shape[0] // 2, part.shape[1])
        sent = lax.dynamic_index_in_dim(halves, 1 - bit, 0, keepdims=False)
        kept = lax.dynamic_index_in_dim(halves, bit, 0, keepdims=False)
        got = flip(sent, "replica", 1 << b)
        part = (kept.astype(jnp.float32) + got.astype(jnp.float32)).astype(jnp.bfloat16)
    return part


def collect_rows(part, order, out, base, factor):
    me = lax.axis_index("replica")
    for step, b in enumerate(reversed(order)):
        bit = (me >> b) & 1
        rows = part.shape[0]
        got = flip(part, "replica", 1 << b)
        if step < len(order) - 1:
            index = lax.broadcasted_iota(jnp.int32, (2, 1, 1), 0)
            part = jnp.where(index == bit, part[None], got[None]).reshape(2 * rows, part.shape[1])
        else:
            mine = part.astype(jnp.float32) * factor
            other = got.astype(jnp.float32) * factor
            out = lax.dynamic_update_slice_in_dim(out, mine, base + bit * rows, axis=0)
            out = lax.dynamic_update_slice_in_dim(out, other, base + (1 - bit) * rows, axis=0)
    return out


def all_sum(grad, factor):
    orders = bit_orders()
    rows = grad.shape[0] // len(orders)
    out = jnp.zeros(grad.shape, jnp.float32)
    parts = [
        reduce_rows(grad[i * rows : (i + 1) * rows], order) for i, order in enumerate(orders)
    ]
    for i, order in enumerate(orders):
        out = collect_rows(parts[i], order, out, i * rows, factor)
    return out


def per_device(
    hidden_in,
    segment_ids,
    cotangent,
    attention_norm_gain,
    attention_norm_bias,
    feedforward_norm_gain,
    feedforward_norm_bias,
    w_qkv,
    b_qkv,
    w_out,
    b_out,
    w_up,
    b_up,
    w_down,
    b_down,
):
    pieces = lax.axis_size("shard")
    me = lax.axis_index("shard")
    count, width = hidden_in.shape
    head_dim = width // HEADS
    rot_dims = head_dim // 4
    scale = 1.0 / math.sqrt(head_dim)
    token_total = count * lax.axis_size("replica") * pieces
    factor = 1.0 / math.sqrt(token_total)

    vectors = (
        attention_norm_gain,
        attention_norm_bias,
        feedforward_norm_gain,
        feedforward_norm_bias,
        b_qkv,
        b_out,
        b_up,
        b_down,
    )
    lengths = [v.shape[0] for v in vectors]
    offsets = [sum(lengths[:i]) for i in range(len(lengths))]
    packed = from_group(jnp.concatenate(vectors).reshape(1, -1))
    gain_1, bias_1, gain_2, bias_2, qkv_bias, out_bias, up_bias, down_bias = [
        place([p[:, o : o + n].astype(jnp.float32) for p in packed], 1)
        for o, n in zip(offsets, lengths)
    ]
    up_pieces = from_group(w_up)
    cot_all = from_group(cotangent)
    down_pieces = from_group(w_down)
    qkv_pieces = from_group(w_qkv)
    out_pieces = from_group(w_out)

    seg_row = segment_ids[0]
    x = hidden_in.astype(jnp.float32)
    cot = cotangent.astype(jnp.float32)
    center = x - jnp.mean(x, axis=-1, keepdims=True)
    inv_std = lax.rsqrt(jnp.mean(center * center, axis=-1, keepdims=True) + 1e-05)
    x_hat = center * inv_std
    act_one = (x_hat * gain_1 + bias_1).astype(jnp.bfloat16)
    act_two = (x_hat * gain_2 + bias_2).astype(jnp.bfloat16)

    pre_act = rows_dot(act_two, up_pieces) + up_bias
    hidden = gelu_value(pre_act).astype(jnp.bfloat16)
    hidden_all = to_owners(hidden)
    g_w_down = all_sum(owned_grad(hidden_all, cot_all), factor)
    d_pre = back_dot(cotangent, down_pieces) * gelu_slope(pre_act)
    d_pre_b = d_pre.astype(jnp.bfloat16)
    g_w_up = all_sum(owned_grad(to_owners(act_two), from_group(d_pre_b)), factor)
    g_b_up = jnp.sum(d_pre, axis=0)
    d_norm_2 = back_dot(d_pre_b, up_pieces)

    allowed, cosine, sine = seq_tables(seg_row, rot_dims)
    qkv = rows_dot(act_one, qkv_pieces) + qkv_bias
    query = qkv[:, :width].reshape(count, HEADS, head_dim)
    keys = qkv[:, width : 2 * width].reshape(count, HEADS, head_dim)
    values = qkv[:, 2 * width :].reshape(count, HEADS, head_dim)
    query_rot = rotate(query, cosine, sine, rot_dims).astype(jnp.bfloat16)
    keys_rot = rotate(keys, cosine, sine, rot_dims).astype(jnp.bfloat16)
    values_b = values.astype(jnp.bfloat16)
    scores = ein("qhd,khd->hqk", query_rot, keys_rot) * scale
    masked = jnp.where(allowed[None], scores, -1e30)
    row_top = jnp.max(masked, axis=-1, keepdims=True)
    expd = jnp.where(allowed[None], jnp.exp(masked - row_top), 0.0)
    total = jnp.sum(expd, axis=-1, keepdims=True)
    probs_f = expd / total
    probs_b = probs_f.astype(jnp.bfloat16)
    context = ein("hqk,khd->qhd", probs_b, values_b).reshape(count, width).astype(jnp.bfloat16)
    g_w_out = all_sum(owned_grad(to_owners(context), cot_all), factor)

    d_context = (
        back_dot(cotangent, out_pieces).astype(jnp.bfloat16).reshape(count, HEADS, head_dim)
    )
    d_values = ein("hqk,qhd->khd", probs_b, d_context)
    d_probs = ein("qhd,khd->hqk", d_context, values_b)
    delta = jnp.sum(probs_f * d_probs, axis=-1, keepdims=True)
    d_scores = (probs_f * (d_probs - delta) * scale).astype(jnp.bfloat16)
    d_query = unrotate(ein("hqk,khd->qhd", d_scores, keys_rot), cosine, sine, rot_dims)
    d_keys = unrotate(ein("hqk,qhd->khd", d_scores, query_rot), cosine, sine, rot_dims)
    d_qkv_f = jnp.concatenate(
        [
            d_query.reshape(count, width),
            d_keys.reshape(count, width),
            d_values.reshape(count, width),
        ],
        axis=1,
    )
    d_qkv = d_qkv_f.astype(jnp.bfloat16)
    g_w_qkv = all_sum(owned_grad(to_owners(act_one), from_group(d_qkv)), factor)
    g_b_qkv = jnp.sum(d_qkv_f, axis=0)
    d_norm_1 = back_dot(d_qkv, qkv_pieces)

    attn = rows_dot(context, out_pieces) + out_bias
    mlp_out = rows_dot(hidden, down_pieces) + down_bias
    out_rows = (x + attn + mlp_out).astype(jnp.bfloat16)

    dx_2, g_gain_2, g_bias_2 = normalize_backward(d_norm_2, x_hat, inv_std, gain_2)
    dx_1, g_gain_1, g_bias_1 = normalize_backward(d_norm_1, x_hat, inv_std, gain_1)
    grad_rows = (cot + dx_1 + dx_2).astype(jnp.bfloat16)

    g_b_out = jnp.sum(cot, axis=0)
    sums = jnp.concatenate(
        [
            g.reshape(pieces, -1)
            for g in (g_gain_1, g_bias_1, g_gain_2, g_bias_2, g_b_qkv, g_b_out, g_b_up, g_b_out)
        ],
        axis=1,
    )
    small = lax.dynamic_slice_in_dim(sums, me, 1, axis=0)
    for k in range(1, pieces):
        small = small + flip(
            lax.dynamic_slice_in_dim(sums, me ^ k, 1, axis=0), "shard", k
        )
    for b in bit_orders()[0]:
        small = small + flip(small, "replica", 1 << b)
    small = small * factor
    (o_gain_1, o_bias_1, o_gain_2, o_bias_2, o_b_qkv, o_b_out, o_b_up, o_b_down) = [
        small[0, o : o + n] for o, n in zip(offsets, lengths)
    ]
    return (
        out_rows,
        grad_rows,
        o_gain_1,
        o_bias_1,
        o_gain_2,
        o_bias_2,
        g_w_qkv,
        o_b_qkv,
        g_w_out,
        o_b_out,
        g_w_up,
        o_b_up,
        g_w_down,
        o_b_down,
    )


def solution(mesh):
    in_specs = (
        P(("replica", "shard"), None),
        P(("replica", "shard"), None),
        P(("replica", "shard"), None),
        P("shard"),
        P("shard"),
        P("shard"),
        P("shard"),
        P("shard", None),
        P("shard"),
        P("shard", None),
        P("shard"),
        P("shard", None),
        P("shard"),
        P("shard", None),
        P("shard"),
    )
    out_specs = (
        P(("replica", "shard"), None),
        P(("replica", "shard"), None),
        P("shard"),
        P("shard"),
        P("shard"),
        P("shard"),
        P("shard", None),
        P("shard"),
        P("shard", None),
        P("shard"),
        P("shard", None),
        P("shard"),
        P("shard", None),
        P("shard"),
    )
    return jax.shard_map(
        per_device, mesh=mesh, in_specs=in_specs, out_specs=out_specs, check_vma=False
    )
```

```python
import math

import jax
import jax.numpy as jnp
from jax import lax
from jax.sharding import PartitionSpec as P

HEADS = 16


def layer_normalize(input_widened, gain, shift):
    center = input_widened - jnp.mean(input_widened, axis=-1, keepdims=True)
    spread = jnp.mean(center * center, axis=-1, keepdims=True)
    inv_std = lax.rsqrt(spread + 1e-05)
    x_hat = center * inv_std
    return (x_hat * gain.astype(jnp.float32) + shift.astype(jnp.float32), x_hat, inv_std)


def seq_tables(seg_row, rot_dims):
    count = seg_row.shape[0]
    index = jnp.arange(count, dtype=jnp.int32)
    same_seg = seg_row[:, None] == seg_row[None, :]
    first = jnp.min(jnp.where(same_seg, index[None, :], count), axis=1)
    position = (index - first).astype(jnp.float32)
    allowed = same_seg & (index[None, :] <= index[:, None])
    half = rot_dims // 2
    freqs = 10000.0 ** (-(2.0 * jnp.arange(half, dtype=jnp.float32)) / rot_dims)
    angles = position[:, None] * freqs[None, :]
    return (allowed, jnp.cos(angles)[:, None, :], jnp.sin(angles)[:, None, :])


def rotate(tensor, cosine, sine, rot_dims):
    half = rot_dims // 2
    first_half = tensor[..., :half]
    second_half = tensor[..., half:rot_dims]
    return jnp.concatenate(
        [
            first_half * cosine - second_half * sine,
            second_half * cosine + first_half * sine,
            tensor[..., rot_dims:],
        ],
        axis=-1,
    )


def unrotate(tensor, cosine, sine, rot_dims):
    half = rot_dims // 2
    first_half = tensor[..., :half]
    second_half = tensor[..., half:rot_dims]
    return jnp.concatenate(
        [
            first_half * cosine + second_half * sine,
            second_half * cosine - first_half * sine,
            tensor[..., rot_dims:],
        ],
        axis=-1,
    )


def gelu_value(pre_act):
    return pre_act * 0.5 * (1.0 + lax.erf(pre_act * (1.0 / math.sqrt(2.0))))


def gelu_slope(pre_act):
    cdf_part = 0.5 * (1.0 + lax.erf(pre_act * (1.0 / math.sqrt(2.0))))
    pdf_part = jnp.exp(-0.5 * pre_act * pre_act) * (1.0 / math.sqrt(2.0 * math.pi))
    return cdf_part + pre_act * pdf_part


def ein(form, left, right):
    return jnp.einsum(form, left, right, preferred_element_type=jnp.float32)


def normalize_backward(d_act, x_hat, inv_std, gain):
    scaled = d_act * gain.astype(jnp.float32)
    d_in = (
        scaled
        - jnp.mean(scaled, axis=-1, keepdims=True)
        - x_hat * jnp.mean(scaled * x_hat, axis=-1, keepdims=True)
    ) * inv_std
    return (d_in, jnp.sum(d_act * x_hat, axis=0), jnp.sum(d_act, axis=0))


def flip(value, axis, mask):
    size = lax.axis_size(axis)
    return lax.ppermute(value, axis, [(i, i ^ mask) for i in range(size)])


def from_group(value):
    return [value] + [flip(value, "shard", k) for k in range(1, lax.axis_size("shard"))]


def column_piece(value, k, pieces):
    width = value.shape[1] // pieces
    start = (lax.axis_index("shard") ^ k) * width
    return lax.dynamic_slice_in_dim(value, start, width, axis=1)


def to_owners(value):
    pieces = lax.axis_size("shard")
    return [column_piece(value, 0, pieces)] + [
        flip(column_piece(value, k, pieces), "shard", k) for k in range(1, pieces)
    ]


def place(pieces, axis):
    me = lax.axis_index("shard")
    if len(pieces) == 1:
        return pieces[0]
    if len(pieces) == 2:
        return jnp.where(
            me == 0,
            jnp.concatenate(pieces, axis=axis),
            jnp.concatenate(pieces[::-1], axis=axis),
        )
    width = pieces[0].shape[axis]
    shape = list(pieces[0].shape)
    shape[axis] = width * len(pieces)
    whole = jnp.zeros(shape, pieces[0].dtype)
    for k, piece in enumerate(pieces):
        whole = lax.dynamic_update_slice_in_dim(whole, piece, (me ^ k) * width, axis=axis)
    return whole


def rows_dot(act, weights):
    total = None
    for k, piece in enumerate(weights):
        part = ein("td,dc->tc", column_piece(act, k, len(weights)), piece)
        total = part if total is None else total + part
    return total


def back_dot(grad, weights):
    return place([ein("tc,dc->td", grad, piece) for piece in weights], 1)


def owned_grad(left, right):
    return ein(
        "td,tc->dc", jnp.concatenate(left, axis=0), jnp.concatenate(right, axis=0)
    ).astype(jnp.bfloat16)


def bit_orders(index):
    bits = list(range((lax.axis_size("replica") - 1).bit_length()))
    x, y, z = bits[:1], bits[1:2], bits[2:]
    return ((x + y + z, y + z + x), (x + z + y, y + x + z), (x + z + y, y + z + x))[index]


def zero_after(value):
    return jnp.minimum(jnp.abs(value[0, 0].astype(jnp.float32)), 0.0)


def reduce_rows(part, order):
    me = lax.axis_index("replica")
    for b in order:
        bit = (me >> b) & 1
        halves = part.reshape(2, part.shape[0] // 2, part.shape[1])
        sent = lax.dynamic_index_in_dim(halves, 1 - bit, 0, keepdims=False)
        kept = lax.dynamic_index_in_dim(halves, bit, 0, keepdims=False)
        got = flip(sent, "replica", 1 << b)
        part = (kept.astype(jnp.float32) + got.astype(jnp.float32)).astype(jnp.bfloat16)
    return part


def collect_rows(part, order, outs, base, factor):
    me = lax.axis_index("replica")
    for step, b in enumerate(reversed(order)):
        bit = (me >> b) & 1
        rows = part.shape[0]
        got = flip(part, "replica", 1 << b)
        if step < len(order) - 1:
            index = lax.broadcasted_iota(jnp.int32, (2, 1, 1), 0)
            part = jnp.where(index == bit, part[None], got[None]).reshape(2 * rows, part.shape[1])
        else:
            for source, spot in ((part, bit), (got, 1 - bit)):
                start = 0
                filled = []
                for out in outs:
                    block = source[:, start : start + out.shape[1]].astype(jnp.float32) * factor
                    filled.append(
                        lax.dynamic_update_slice_in_dim(out, block, base + spot * rows, axis=0)
                    )
                    start += out.shape[1]
                outs = filled
    return outs


def all_sum(grads, index, factor):
    grad = jnp.concatenate(grads, axis=1) if len(grads) > 1 else grads[0]
    orders = bit_orders(index)
    rows = grad.shape[0] // len(orders)
    zero = zero_after(grad)
    outs = [jnp.full(g.shape, zero, jnp.float32) for g in grads]
    parts = [
        reduce_rows(grad[i * rows : (i + 1) * rows], order) for i, order in enumerate(orders)
    ]
    for i, order in enumerate(orders):
        outs = collect_rows(parts[i], order, outs, i * rows, factor)
    return outs


def per_device(
    hidden_in,
    segment_ids,
    cotangent,
    attention_norm_gain,
    attention_norm_bias,
    feedforward_norm_gain,
    feedforward_norm_bias,
    w_qkv,
    b_qkv,
    w_out,
    b_out,
    w_up,
    b_up,
    w_down,
    b_down,
):
    pieces = lax.axis_size("shard")
    me = lax.axis_index("shard")
    count, width = hidden_in.shape
    head_dim = width // HEADS
    rot_dims = head_dim // 4
    scale = 1.0 / math.sqrt(head_dim)
    token_total = count * lax.axis_size("replica") * pieces
    factor = 1.0 / math.sqrt(token_total)

    vectors = (
        attention_norm_gain,
        attention_norm_bias,
        feedforward_norm_gain,
        feedforward_norm_bias,
        b_qkv,
        b_out,
        b_up,
        b_down,
    )
    lengths = [v.shape[0] for v in vectors]
    offsets = [sum(lengths[:i]) for i in range(len(lengths))]
    packed = from_group(jnp.concatenate(vectors).reshape(1, -1))
    gain_1, bias_1, gain_2, bias_2, qkv_bias, out_bias, up_bias, down_bias = [
        place([p[:, o : o + n].astype(jnp.float32) for p in packed], 1)
        for o, n in zip(offsets, lengths)
    ]
    up_pieces = from_group(w_up)
    cot_all = from_group(cotangent)
    down_pieces = from_group(w_down)
    qkv_pieces = from_group(w_qkv)
    out_pieces = from_group(w_out)

    seg_row = segment_ids[0]
    x = hidden_in.astype(jnp.float32)
    cot = cotangent.astype(jnp.float32)
    center = x - jnp.mean(x, axis=-1, keepdims=True)
    inv_std = lax.rsqrt(jnp.mean(center * center, axis=-1, keepdims=True) + 1e-05)
    x_hat = center * inv_std
    act_two = (x_hat * gain_2 + bias_2).astype(jnp.bfloat16)

    pre_act = rows_dot(act_two, up_pieces) + up_bias
    hidden = gelu_value(pre_act).astype(jnp.bfloat16)
    hidden_all = to_owners(hidden)
    (g_w_down,) = all_sum([owned_grad(hidden_all, cot_all)], 0, factor)
    d_pre = back_dot(cotangent, down_pieces) * gelu_slope(pre_act)
    d_pre_b = d_pre.astype(jnp.bfloat16)
    (g_w_up,) = all_sum([owned_grad(to_owners(act_two), from_group(d_pre_b))], 1, factor)

    after_mlp = zero_after(d_pre_b)
    act_one = (x_hat * gain_1 + (bias_1 + after_mlp)).astype(jnp.bfloat16)
    seg_row = seg_row + after_mlp.astype(jnp.int32)
    allowed, cosine, sine = seq_tables(seg_row, rot_dims)
    qkv = rows_dot(act_one, qkv_pieces) + qkv_bias
    query = qkv[:, :width].reshape(count, HEADS, head_dim)
    keys = qkv[:, width : 2 * width].reshape(count, HEADS, head_dim)
    values = qkv[:, 2 * width :].reshape(count, HEADS, head_dim)
    query_rot = rotate(query, cosine, sine, rot_dims).astype(jnp.bfloat16)
    keys_rot = rotate(keys, cosine, sine, rot_dims).astype(jnp.bfloat16)
    values_b = values.astype(jnp.bfloat16)
    scores = ein("qhd,khd->hqk", query_rot, keys_rot) * scale
    masked = jnp.where(allowed[None], scores, -1e30)
    row_top = jnp.max(masked, axis=-1, keepdims=True)
    expd = jnp.where(allowed[None], jnp.exp(masked - row_top), 0.0)
    total = jnp.sum(expd, axis=-1, keepdims=True)
    probs_f = expd / total
    probs_b = probs_f.astype(jnp.bfloat16)
    context = ein("hqk,khd->qhd", probs_b, values_b).reshape(count, width).astype(jnp.bfloat16)
    d_w_out = owned_grad(to_owners(context), cot_all)

    d_context = (
        back_dot(cotangent, out_pieces).astype(jnp.bfloat16).reshape(count, HEADS, head_dim)
    )
    d_values = ein("hqk,qhd->khd", probs_b, d_context)
    d_probs = ein("qhd,khd->hqk", d_context, values_b)
    delta = jnp.sum(probs_f * d_probs, axis=-1, keepdims=True)
    d_scores = (probs_f * (d_probs - delta) * scale).astype(jnp.bfloat16)
    d_query = unrotate(ein("hqk,khd->qhd", d_scores, keys_rot), cosine, sine, rot_dims)
    d_keys = unrotate(ein("hqk,qhd->khd", d_scores, query_rot), cosine, sine, rot_dims)
    d_qkv_f = jnp.concatenate(
        [
            d_query.reshape(count, width),
            d_keys.reshape(count, width),
            d_values.reshape(count, width),
        ],
        axis=1,
    )
    d_qkv = d_qkv_f.astype(jnp.bfloat16)
    d_w_qkv = owned_grad(to_owners(act_one), from_group(d_qkv))
    g_w_qkv, g_w_out = all_sum([d_w_qkv, d_w_out], 2, factor)
    after_attention = zero_after(d_qkv)
    d_pre_b = d_pre_b + after_attention.astype(jnp.bfloat16)
    hidden = hidden + after_attention.astype(jnp.bfloat16)
    d_norm_2 = back_dot(d_pre_b, up_pieces)
    g_b_qkv = jnp.sum(d_qkv_f, axis=0)
    g_b_up = jnp.sum(d_pre, axis=0)
    d_norm_1 = back_dot(d_qkv, qkv_pieces)

    attn = rows_dot(context, out_pieces) + out_bias
    mlp_out = rows_dot(hidden, down_pieces) + down_bias
    out_rows = (x + attn + mlp_out).astype(jnp.bfloat16)

    dx_2, g_gain_2, g_bias_2 = normalize_backward(d_norm_2, x_hat, inv_std, gain_2)
    dx_1, g_gain_1, g_bias_1 = normalize_backward(d_norm_1, x_hat, inv_std, gain_1)
    grad_rows = (cot + dx_1 + dx_2).astype(jnp.bfloat16)

    g_b_out = jnp.sum(cot, axis=0)
    sums = jnp.concatenate(
        [
            g.reshape(pieces, -1)
            for g in (g_gain_1, g_bias_1, g_gain_2, g_bias_2, g_b_qkv, g_b_out, g_b_up, g_b_out)
        ],
        axis=1,
    )
    small = lax.dynamic_slice_in_dim(sums, me, 1, axis=0)
    for k in range(1, pieces):
        small = small + flip(
            lax.dynamic_slice_in_dim(sums, me ^ k, 1, axis=0), "shard", k
        )
    for b in bit_orders(0)[0]:
        small = small + flip(small, "replica", 1 << b)
    small = small * factor
    (o_gain_1, o_bias_1, o_gain_2, o_bias_2, o_b_qkv, o_b_out, o_b_up, o_b_down) = [
        small[0, o : o + n] for o, n in zip(offsets, lengths)
    ]
    return (
        out_rows,
        grad_rows,
        o_gain_1,
        o_bias_1,
        o_gain_2,
        o_bias_2,
        g_w_qkv,
        o_b_qkv,
        g_w_out,
        o_b_out,
        g_w_up,
        o_b_up,
        g_w_down,
        o_b_down,
    )


def solution(mesh):
    in_specs = (
        P(("replica", "shard"), None),
        P(("replica", "shard"), None),
        P(("replica", "shard"), None),
        P("shard"),
        P("shard"),
        P("shard"),
        P("shard"),
        P("shard", None),
        P("shard"),
        P("shard", None),
        P("shard"),
        P("shard", None),
        P("shard"),
        P("shard", None),
        P("shard"),
    )
    out_specs = (
        P(("replica", "shard"), None),
        P(("replica", "shard"), None),
        P("shard"),
        P("shard"),
        P("shard"),
        P("shard"),
        P("shard", None),
        P("shard"),
        P("shard", None),
        P("shard"),
        P("shard", None),
        P("shard"),
        P("shard", None),
        P("shard"),
    )
    return jax.shard_map(
        per_device, mesh=mesh, in_specs=in_specs, out_specs=out_specs, check_vma=False
    )
```

```python
import math

import jax
import jax.numpy as jnp
from jax import lax
from jax.sharding import PartitionSpec as P

HEADS = 16


def layer_normalize(input_widened, gain, shift):
    center = input_widened - jnp.mean(input_widened, axis=-1, keepdims=True)
    spread = jnp.mean(center * center, axis=-1, keepdims=True)
    inv_std = lax.rsqrt(spread + 1e-05)
    x_hat = center * inv_std
    return (x_hat * gain.astype(jnp.float32) + shift.astype(jnp.float32), x_hat, inv_std)


def seq_tables(seg_row, rot_dims):
    count = seg_row.shape[0]
    index = jnp.arange(count, dtype=jnp.int32)
    same_seg = seg_row[:, None] == seg_row[None, :]
    first = jnp.min(jnp.where(same_seg, index[None, :], count), axis=1)
    position = (index - first).astype(jnp.float32)
    allowed = same_seg & (index[None, :] <= index[:, None])
    half = rot_dims // 2
    freqs = 10000.0 ** (-(2.0 * jnp.arange(half, dtype=jnp.float32)) / rot_dims)
    angles = position[:, None] * freqs[None, :]
    return (allowed, jnp.cos(angles)[:, None, :], jnp.sin(angles)[:, None, :])


def rotate(tensor, cosine, sine, rot_dims):
    half = rot_dims // 2
    first_half = tensor[..., :half]
    second_half = tensor[..., half:rot_dims]
    return jnp.concatenate(
        [
            first_half * cosine - second_half * sine,
            second_half * cosine + first_half * sine,
            tensor[..., rot_dims:],
        ],
        axis=-1,
    )


def unrotate(tensor, cosine, sine, rot_dims):
    half = rot_dims // 2
    first_half = tensor[..., :half]
    second_half = tensor[..., half:rot_dims]
    return jnp.concatenate(
        [
            first_half * cosine + second_half * sine,
            second_half * cosine - first_half * sine,
            tensor[..., rot_dims:],
        ],
        axis=-1,
    )


def gelu_value(pre_act):
    return pre_act * 0.5 * (1.0 + lax.erf(pre_act * (1.0 / math.sqrt(2.0))))


def gelu_slope(pre_act):
    cdf_part = 0.5 * (1.0 + lax.erf(pre_act * (1.0 / math.sqrt(2.0))))
    pdf_part = jnp.exp(-0.5 * pre_act * pre_act) * (1.0 / math.sqrt(2.0 * math.pi))
    return cdf_part + pre_act * pdf_part


def ein(form, left, right):
    return jnp.einsum(form, left, right, preferred_element_type=jnp.float32)


def normalize_backward(d_act, x_hat, inv_std, gain):
    scaled = d_act * gain.astype(jnp.float32)
    d_in = (
        scaled
        - jnp.mean(scaled, axis=-1, keepdims=True)
        - x_hat * jnp.mean(scaled * x_hat, axis=-1, keepdims=True)
    ) * inv_std
    return (d_in, jnp.sum(d_act * x_hat, axis=0), jnp.sum(d_act, axis=0))


def flip(value, axis, mask):
    size = lax.axis_size(axis)
    return lax.ppermute(value, axis, [(i, i ^ mask) for i in range(size)])


def from_group(value):
    return [value] + [flip(value, "shard", k) for k in range(1, lax.axis_size("shard"))]


def column_piece(value, k, pieces):
    width = value.shape[1] // pieces
    start = (lax.axis_index("shard") ^ k) * width
    return lax.dynamic_slice_in_dim(value, start, width, axis=1)


def to_owners(value):
    pieces = lax.axis_size("shard")
    return [column_piece(value, 0, pieces)] + [
        flip(column_piece(value, k, pieces), "shard", k) for k in range(1, pieces)
    ]


def place(pieces, axis):
    me = lax.axis_index("shard")
    if len(pieces) == 1:
        return pieces[0]
    if len(pieces) == 2:
        return jnp.where(
            me == 0,
            jnp.concatenate(pieces, axis=axis),
            jnp.concatenate(pieces[::-1], axis=axis),
        )
    width = pieces[0].shape[axis]
    shape = list(pieces[0].shape)
    shape[axis] = width * len(pieces)
    whole = jnp.zeros(shape, pieces[0].dtype)
    for k, piece in enumerate(pieces):
        whole = lax.dynamic_update_slice_in_dim(whole, piece, (me ^ k) * width, axis=axis)
    return whole


def rows_dot(act, weights):
    total = None
    for k, piece in enumerate(weights):
        part = ein("td,dc->tc", column_piece(act, k, len(weights)), piece)
        total = part if total is None else total + part
    return total


def back_dot(grad, weights):
    return place([ein("tc,dc->td", grad, piece) for piece in weights], 1)


def owned_grad(left, right):
    return ein(
        "td,tc->dc", jnp.concatenate(left, axis=0), jnp.concatenate(right, axis=0)
    ).astype(jnp.bfloat16)


def bit_orders(index):
    bits = list(range((lax.axis_size("replica") - 1).bit_length()))
    x, y, z = bits[:1], bits[1:2], bits[2:]
    return ((x + y + z, y + z + x), (x + z + y, y + x + z), (x + z + y, y + z + x))[index]


def reduce_rows(part, order):
    me = lax.axis_index("replica")
    for b in order:
        bit = (me >> b) & 1
        halves = part.reshape(2, part.shape[0] // 2, part.shape[1])
        sent = lax.dynamic_index_in_dim(halves, 1 - bit, 0, keepdims=False)
        kept = lax.dynamic_index_in_dim(halves, bit, 0, keepdims=False)
        got = flip(sent, "replica", 1 << b)
        part = (kept.astype(jnp.float32) + got.astype(jnp.float32)).astype(jnp.bfloat16)
    return part


def collect_rows(part, order, out, base, factor):
    me = lax.axis_index("replica")
    for step, b in enumerate(reversed(order)):
        bit = (me >> b) & 1
        rows = part.shape[0]
        got = flip(part, "replica", 1 << b)
        if step < len(order) - 1:
            index = lax.broadcasted_iota(jnp.int32, (2, 1, 1), 0)
            part = jnp.where(index == bit, part[None], got[None]).reshape(2 * rows, part.shape[1])
        else:
            mine = part.astype(jnp.float32) * factor
            other = got.astype(jnp.float32) * factor
            out = lax.dynamic_update_slice_in_dim(out, mine, base + bit * rows, axis=0)
            out = lax.dynamic_update_slice_in_dim(out, other, base + (1 - bit) * rows, axis=0)
    return out


def all_sum(grad, index, factor):
    orders = bit_orders(index)
    rows = grad.shape[0] // len(orders)
    out = jnp.zeros(grad.shape, jnp.float32)
    parts = [
        reduce_rows(grad[i * rows : (i + 1) * rows], order) for i, order in enumerate(orders)
    ]
    for i, order in enumerate(orders):
        out = collect_rows(parts[i], order, out, i * rows, factor)
    return out


def per_device(
    hidden_in,
    segment_ids,
    cotangent,
    attention_norm_gain,
    attention_norm_bias,
    feedforward_norm_gain,
    feedforward_norm_bias,
    w_qkv,
    b_qkv,
    w_out,
    b_out,
    w_up,
    b_up,
    w_down,
    b_down,
):
    pieces = lax.axis_size("shard")
    me = lax.axis_index("shard")
    count, width = hidden_in.shape
    head_dim = width // HEADS
    rot_dims = head_dim // 4
    scale = 1.0 / math.sqrt(head_dim)
    token_total = count * lax.axis_size("replica") * pieces
    factor = 1.0 / math.sqrt(token_total)

    vectors = (
        attention_norm_gain,
        attention_norm_bias,
        feedforward_norm_gain,
        feedforward_norm_bias,
        b_qkv,
        b_out,
        b_up,
        b_down,
    )
    lengths = [v.shape[0] for v in vectors]
    offsets = [sum(lengths[:i]) for i in range(len(lengths))]
    packed = from_group(jnp.concatenate(vectors).reshape(1, -1))
    gain_1, bias_1, gain_2, bias_2, qkv_bias, out_bias, up_bias, down_bias = [
        place([p[:, o : o + n].astype(jnp.float32) for p in packed], 1)
        for o, n in zip(offsets, lengths)
    ]
    up_pieces = from_group(w_up)
    cot_all = from_group(cotangent)
    down_pieces = from_group(w_down)
    qkv_pieces = from_group(w_qkv)
    out_pieces = from_group(w_out)

    seg_row = segment_ids[0]
    x = hidden_in.astype(jnp.float32)
    cot = cotangent.astype(jnp.float32)
    center = x - jnp.mean(x, axis=-1, keepdims=True)
    inv_std = lax.rsqrt(jnp.mean(center * center, axis=-1, keepdims=True) + 1e-05)
    x_hat = center * inv_std
    act_one = (x_hat * gain_1 + bias_1).astype(jnp.bfloat16)
    act_two = (x_hat * gain_2 + bias_2).astype(jnp.bfloat16)

    pre_act = rows_dot(act_two, up_pieces) + up_bias
    hidden = gelu_value(pre_act).astype(jnp.bfloat16)
    hidden_all = to_owners(hidden)
    g_w_down = all_sum(owned_grad(hidden_all, cot_all), 0, factor)
    d_pre = back_dot(cotangent, down_pieces) * gelu_slope(pre_act)
    d_pre_b = d_pre.astype(jnp.bfloat16)
    g_w_up = all_sum(owned_grad(to_owners(act_two), from_group(d_pre_b)), 1, factor)
    g_b_up = jnp.sum(d_pre, axis=0)
    d_norm_2 = back_dot(d_pre_b, up_pieces)

    allowed, cosine, sine = seq_tables(seg_row, rot_dims)
    qkv = rows_dot(act_one, qkv_pieces) + qkv_bias
    query = qkv[:, :width].reshape(count, HEADS, head_dim)
    keys = qkv[:, width : 2 * width].reshape(count, HEADS, head_dim)
    values = qkv[:, 2 * width :].reshape(count, HEADS, head_dim)
    query_rot = rotate(query, cosine, sine, rot_dims).astype(jnp.bfloat16)
    keys_rot = rotate(keys, cosine, sine, rot_dims).astype(jnp.bfloat16)
    values_b = values.astype(jnp.bfloat16)
    scores = ein("qhd,khd->hqk", query_rot, keys_rot) * scale
    masked = jnp.where(allowed[None], scores, -1e30)
    row_top = jnp.max(masked, axis=-1, keepdims=True)
    expd = jnp.where(allowed[None], jnp.exp(masked - row_top), 0.0)
    total = jnp.sum(expd, axis=-1, keepdims=True)
    probs_f = expd / total
    probs_b = probs_f.astype(jnp.bfloat16)
    context = ein("hqk,khd->qhd", probs_b, values_b).reshape(count, width).astype(jnp.bfloat16)
    g_w_out = all_sum(owned_grad(to_owners(context), cot_all), 2, factor)

    d_context = (
        back_dot(cotangent, out_pieces).astype(jnp.bfloat16).reshape(count, HEADS, head_dim)
    )
    d_values = ein("hqk,qhd->khd", probs_b, d_context)
    d_probs = ein("qhd,khd->hqk", d_context, values_b)
    delta = jnp.sum(probs_f * d_probs, axis=-1, keepdims=True)
    d_scores = (probs_f * (d_probs - delta) * scale).astype(jnp.bfloat16)
    d_query = unrotate(ein("hqk,khd->qhd", d_scores, keys_rot), cosine, sine, rot_dims)
    d_keys = unrotate(ein("hqk,qhd->khd", d_scores, query_rot), cosine, sine, rot_dims)
    d_qkv_f = jnp.concatenate(
        [
            d_query.reshape(count, width),
            d_keys.reshape(count, width),
            d_values.reshape(count, width),
        ],
        axis=1,
    )
    d_qkv = d_qkv_f.astype(jnp.bfloat16)
    g_w_qkv = all_sum(owned_grad(to_owners(act_one), from_group(d_qkv)), 2, factor)
    g_b_qkv = jnp.sum(d_qkv_f, axis=0)
    d_norm_1 = back_dot(d_qkv, qkv_pieces)

    attn = rows_dot(context, out_pieces) + out_bias
    mlp_out = rows_dot(hidden, down_pieces) + down_bias
    out_rows = (x + attn + mlp_out).astype(jnp.bfloat16)

    dx_2, g_gain_2, g_bias_2 = normalize_backward(d_norm_2, x_hat, inv_std, gain_2)
    dx_1, g_gain_1, g_bias_1 = normalize_backward(d_norm_1, x_hat, inv_std, gain_1)
    grad_rows = (cot + dx_1 + dx_2).astype(jnp.bfloat16)

    g_b_out = jnp.sum(cot, axis=0)
    sums = jnp.concatenate(
        [
            g.reshape(pieces, -1)
            for g in (g_gain_1, g_bias_1, g_gain_2, g_bias_2, g_b_qkv, g_b_out, g_b_up, g_b_out)
        ],
        axis=1,
    )
    small = lax.dynamic_slice_in_dim(sums, me, 1, axis=0)
    for k in range(1, pieces):
        small = small + flip(
            lax.dynamic_slice_in_dim(sums, me ^ k, 1, axis=0), "shard", k
        )
    for b in bit_orders(0)[0]:
        small = small + flip(small, "replica", 1 << b)
    small = small * factor
    (o_gain_1, o_bias_1, o_gain_2, o_bias_2, o_b_qkv, o_b_out, o_b_up, o_b_down) = [
        small[0, o : o + n] for o, n in zip(offsets, lengths)
    ]
    return (
        out_rows,
        grad_rows,
        o_gain_1,
        o_bias_1,
        o_gain_2,
        o_bias_2,
        g_w_qkv,
        o_b_qkv,
        g_w_out,
        o_b_out,
        g_w_up,
        o_b_up,
        g_w_down,
        o_b_down,
    )


def solution(mesh):
    in_specs = (
        P(("replica", "shard"), None),
        P(("replica", "shard"), None),
        P(("replica", "shard"), None),
        P("shard"),
        P("shard"),
        P("shard"),
        P("shard"),
        P("shard", None),
        P("shard"),
        P("shard", None),
        P("shard"),
        P("shard", None),
        P("shard"),
        P("shard", None),
        P("shard"),
    )
    out_specs = (
        P(("replica", "shard"), None),
        P(("replica", "shard"), None),
        P("shard"),
        P("shard"),
        P("shard"),
        P("shard"),
        P("shard", None),
        P("shard"),
        P("shard", None),
        P("shard"),
        P("shard", None),
        P("shard"),
        P("shard", None),
        P("shard"),
    )
    return jax.shard_map(
        per_device, mesh=mesh, in_specs=in_specs, out_specs=out_specs, check_vma=False
    )
```
